32 devices in a mesh: gx: 2 (over x), gy: 4 (over z), gz: 4 (over y, core).
Axes of the slice: x: 2, y: 2, z: 4, core: 2. Of those that a mesh axis runs over, the one named last changes fastest.
Arguments:
- schur: bfloat16 [2, 4, 4, 1024, 1024], P('gx', 'gy', 'gz'), may hold values from -0.2 to 2.7
- block_map: int32 [2, 4, 4, 26], P('gx', 'gy', 'gz'), may hold values from 0 to 7
- vectors: bfloat16 [2, 4, 4, 1024, 512], P('gx', 'gy', 'gz'), may hold values from -3 to 3
Outputs:
- assembled: bfloat16 [2, 4, 4, 1024, 512], P('gx', 'gy', 'gz')
- update: bfloat16 [2, 4, 4, 1024, 512], P('gx', 'gy', 'gz')
The draws below stay inside these ranges and needn't reach their ends.
All inputs are finite; a program needn't handle non-finite values.
Results may differ from the reference program's by a relative error of at most 0.0056.
Values may be sent and summed in bfloat16 or wider, within the bound.
A program may use at most 64 MiB of HBM per device.

```python
import math
import jax
import jax.numpy as jnp
from jax import lax

NI = 1024
BLOCK = 128
RHS = 512
SLABS = 2
COLUMNS = 4
LAYERS = 4


def draw_schur(key, part):
    first, second = jax.random.split(key)
    full_shape = (SLABS, COLUMNS, LAYERS, NI, NI)
    spread = 1.5 / math.sqrt(NI)
    low_diag = 0.5
    high_diag = 1.5
    coupling = jnp.clip(jax.random.normal(first, full_shape, jnp.float32) * spread, -0.18, 0.18)
    leading = jax.random.uniform(second, full_shape[:4], jnp.float32, low_diag, high_diag)
    identity = jnp.eye(NI, dtype=jnp.float32)
    return (coupling + leading[..., None] * identity).astype(jnp.bfloat16)


def plant(result, stream_key, least, largest):
    longest = result.shape.index(max(result.shape))
    spots = []
    for shift in (0, 1):
        where = [jax.random.randint(jax.random.fold_in(stream_key, axis), (), 0, length) for axis, length in enumerate(result.shape)]
        where[longest] = (where[longest] + shift) % result.shape[longest]
        spots.append(tuple(where))
    return result.at[spots[0]].set(least).at[spots[1]].set(largest)


def levels(stream_key, extent, cuts, smallest, high):
    gain, own = 1.0, jax.random.fold_in(stream_key, 6)
    for position, parts in cuts:
        steps = jnp.exp(jax.random.uniform(jax.random.fold_in(own, position), (parts,), jnp.float32, smallest / len(cuts), high / len(cuts)))
        gain = gain * jnp.repeat(steps, extent[position] // parts).reshape([-1 if axis == position else 1 for axis in range(len(extent))])
    return gain


def bell_draw(key, dims, scale, bound, shards=(), kind=jnp.bfloat16):
    factor_of = levels(key, dims, shards, -0.22, 0.18) if shards else 1.0
    values = jax.random.normal(key, dims, jnp.float32) * scale * factor_of
    return jnp.minimum(jnp.maximum(values, -bound), bound).astype(kind)


def setup_inputs(seed: int = 0) -> dict:
    keys = jax.random.split(jax.random.key(seed), 4)
    schur = draw_schur(jax.random.fold_in(keys[3], 71), 0)
    block_map = plant(jax.random.randint(keys[1], (SLABS, COLUMNS, LAYERS, 26), 0, NI // BLOCK), jax.random.fold_in(keys[1], 1), 0, (NI // BLOCK) - 1).astype(jnp.int32)
    vectors = bell_draw(keys[2], (SLABS, COLUMNS, LAYERS, NI, RHS), 0.5, 3.0, ((0, 2), (1, 4), (2, 4)))
    return {"schur": schur, "block_map": block_map, "vectors": vectors}


def directions():
    return [(a, b, c) for a in (-1, 0, 1) for b in (-1, 0, 1) for c in (-1, 0, 1) if (a, b, c) != (0, 0, 0)]


def reference(schur, block_map, vectors):
    offsets = directions()
    blocks = NI // BLOCK
    total_devices = SLABS * COLUMNS * LAYERS
    flat_schur = schur.reshape(total_devices, NI, NI)
    flat_right = vectors.reshape(total_devices, NI, RHS)

    def multiply(pair):
        return jnp.dot(pair[0], pair[1], preferred_element_type=jnp.float32).astype(jnp.bfloat16)

    product = lax.map(multiply, (flat_schur, flat_right))
    tile_grid = flat_schur.reshape(total_devices, blocks, BLOCK, blocks, BLOCK)
    diagonal = jnp.stack([tile_grid[:, k, :, k, :] for k in range(blocks)], axis=1)
    payload = jnp.concatenate([diagonal, product.reshape(total_devices, blocks, BLOCK, RHS)], axis=3)
    payload_grid = payload.reshape(SLABS, COLUMNS, LAYERS, blocks, BLOCK, BLOCK + RHS)
    labels = jnp.arange(blocks, dtype=jnp.int32)

    def assemble(index):
        p = index // (COLUMNS * LAYERS)
        q = (index // LAYERS) % COLUMNS
        r = index % LAYERS
        totals = payload_grid[p, q, r].astype(jnp.float32)
        counts = jnp.ones((blocks,), jnp.float32)
        for number, (a, b, c) in enumerate(offsets):
            opposite = offsets.index((-a, -b, -c))
            near_p = (p + a) % SLABS
            near_q = q + b
            near_r = r + c
            alive = (near_q >= 0) & (near_q < COLUMNS) & (near_r >= 0) & (near_r < LAYERS)
            near_q = jnp.clip(near_q, 0, COLUMNS - 1)
            near_r = jnp.clip(near_r, 0, LAYERS - 1)
            source = block_map[near_p, near_q, near_r, opposite]
            piece = payload_grid[near_p, near_q, near_r, source].astype(jnp.float32)
            weight = ((labels == block_map[p, q, r, number]) & alive).astype(jnp.float32)
            totals = totals + weight[:, None, None] * piece[None, :, :]
            counts = counts + weight
        coupling = totals[:, :, :BLOCK]
        summed = totals[:, :, BLOCK:]
        scaled = (jnp.einsum("bij,bjk->bik", coupling, summed, precision=lax.Precision.HIGHEST) / counts[:, None, None]).astype(jnp.bfloat16)
        update = jnp.dot(flat_schur[index], scaled.reshape(NI, RHS), preferred_element_type=jnp.float32).astype(jnp.bfloat16)
        return summed.reshape(NI, RHS).astype(jnp.bfloat16), update

    assembled, update = lax.map(assemble, jnp.arange(total_devices, dtype=jnp.int32))
    return assembled.reshape(SLABS, COLUMNS, LAYERS, NI, RHS), update.reshape(SLABS, COLUMNS, LAYERS, NI, RHS)
```

```python
import functools

import jax
import jax.numpy as jnp
from jax import lax
from jax.experimental import pallas as pl
from jax.experimental.pallas import tpu as pltpu
from jax.sharding import PartitionSpec as P

BLOCK = 128
TILE = 32
MESH = pl.DeviceIdType.MESH
DIRS = [
    (a, b, c)
    for a in (-1, 0, 1)
    for b in (-1, 0, 1)
    for c in (-1, 0, 1)
    if (a, b, c) != (0, 0, 0)
]
PLANE = [(b, c) for b in (-1, 0, 1) for c in (-1, 0, 1) if (b, c) != (0, 0)]


def number(a, b, c):
    return DIRS.index((a, b, c))


def kernel(
    sizes,
    widths,
    map_ref,
    schur_hbm,
    vec_hbm,
    asm_hbm,
    upd_hbm,
    schur,
    vec,
    own_w,
    relay_w,
    maps,
    map_out,
    map_in,
    pays,
    parts,
    stages,
    recvs,
    comb,
    comb_in,
    tots,
    scaleds,
    asms,
    upds,
    load_sem,
    store_sem,
    mapc_sem,
    map_send,
    map_recv,
    x_send,
    x_recv,
    p_send,
    p_recv,
    b_send,
    b_recv,
):
    gx, gy, gz = sizes
    order = schur.shape[0]
    blocks = order // BLOCK
    group_rows = 2 * BLOCK
    groups = order // group_rows
    last = len(widths) - 1
    p, q, r = lax.axis_index("gx"), lax.axis_index("gy"), lax.axis_index("gz")
    shifts = (1,) if gx == 2 else (-1, 1)

    def slot(a):
        return 0 if gx == 2 or a == -1 else 1

    def inside(b, c):
        return (q + b >= 0) & (q + b < gy) & (r + c >= 0) & (r + c < gz)

    def across(a):
        return {"gx": lax.rem(p + a + gx, gx), "gy": q, "gz": r}

    def beside(b, c):
        return {"gx": p, "gy": q + b, "gz": r + c}

    barrier = pltpu.get_barrier_semaphore()
    for a in shifts:
        pl.semaphore_signal(barrier, inc=1, device_id=across(a), device_id_type=MESH)
    for b, c in PLANE:

        @pl.when(inside(b, c))
        def _(b=b, c=c):
            pl.semaphore_signal(barrier, inc=1, device_id=beside(b, c), device_id_type=MESH)

    rows_near = 3 - jnp.where(q == 0, 1, 0) - jnp.where(q == gy - 1, 1, 0)
    cols_near = 3 - jnp.where(r == 0, 1, 0) - jnp.where(r == gz - 1, 1, 0)
    peers = rows_near * cols_near - 1 + len(shifts)

    vec_copy = pltpu.make_async_copy(vec_hbm, vec, load_sem.at[groups])
    vec_copy.start()
    loads = []
    for g in range(groups):
        rows = pl.ds(g * group_rows, group_rows)
        load = pltpu.make_async_copy(schur_hbm.at[rows], schur.at[rows], load_sem.at[g])
        load.start()
        loads.append(load)

    lanes = lax.broadcasted_iota(jnp.int32, (8, 128), 1)
    row = jnp.zeros((8, 128), jnp.int32)
    for e in range(26):
        row = jnp.where(lanes == e, map_ref[e], row)
    map_out[...] = row

    for e, (a, b, c) in enumerate(DIRS):
        alive = inside(-b, -c)
        for k in range(blocks):
            hit = (map_ref[25 - e] == k) & alive
            own_w[e * blocks + k] = jnp.where(hit, 1.0, 0.0).astype(jnp.float32)
    for s, (b, c) in enumerate(PLANE):

        @pl.when(jnp.logical_not(inside(-b, -c)))
        def _(s=s):
            for recv in recvs:
                recv[s] = jnp.zeros(recv.shape[1:], recv.dtype)

    def x_copy(j, a, lo, n, sem):
        return pltpu.make_async_remote_copy(
            src_ref=pays[j].at[pl.ds(lo, n)],
            dst_ref=parts[j].at[slot(a), pl.ds(lo, n)],
            send_sem=x_send.at[j, slot(a), sem],
            recv_sem=x_recv.at[j, slot(a), sem],
            device_id=across(a),
            device_id_type=MESH,
        )

    def map_copy(a):
        return pltpu.make_async_remote_copy(
            src_ref=map_out,
            dst_ref=map_in.at[slot(a)],
            send_sem=map_send.at[slot(a)],
            recv_sem=map_recv.at[slot(a)],
            device_id=across(a),
            device_id_type=MESH,
        )

    def plane_copy(j, s):
        b, c = PLANE[s]
        return pltpu.make_async_remote_copy(
            src_ref=stages[j].at[s],
            dst_ref=recvs[j].at[s],
            send_sem=p_send.at[j, s],
            recv_sem=p_recv.at[j, s],
            device_id=beside(b, c),
            device_id_type=MESH,
        )

    def b_copy(a):
        return pltpu.make_async_remote_copy(
            src_ref=comb.at[slot(a)],
            dst_ref=comb_in.at[slot(a)],
            send_sem=b_send.at[slot(a)],
            recv_sem=b_recv.at[slot(a)],
            device_id=across(a),
            device_id_type=MESH,
        )

    vec_copy.wait()
    for g in range(groups):
        loads[g].wait()
        rows = pl.ds(g * group_rows, group_rows)
        product = jnp.dot(schur[rows, :], vec[...], preferred_element_type=jnp.float32)
        product = product.astype(jnp.bfloat16)
        for half in range(2):
            k = 2 * g + half
            part = product[half * BLOCK : (half + 1) * BLOCK]
            spot = pl.ds(k * BLOCK, BLOCK)
            pays[0][k, :, :BLOCK] = schur[spot, spot]
            start = 0
            for j, width in enumerate(widths):
                lead = BLOCK if j == 0 else 0
                pays[j][k, :, lead:] = part[:, start : start + width - lead]
                start += width - lead
        if g == 0:
            pl.semaphore_wait(barrier, peers)

            for a in shifts:
                map_copy(a).start()
        for a in shifts:
            x_copy(0, a, 2 * g, 2, g).start()
    for j in range(1, last):
        for a in shifts:
            x_copy(j, a, 0, blocks, 0).start()

    def stage(j, near):
        for s, (b, c) in enumerate(PLANE):

            @pl.when(inside(b, c))
            def _(s=s, b=b, c=c):
                stages[j][s, 1] = pays[j][map_ref[number(0, b, c)]]
                for place, a in ((0, -1), (2, 1)):
                    if near:
                        stages[j][s, place] = parts[j][
                            slot(a), maps[slot(a), 0, number(a, b, c)]
                        ]
                    else:
                        stages[j][s, place] = pays[j][map_ref[number(a, b, c)]]
                plane_copy(j, s).start()

    def arrived(j):
        for s, (b, c) in enumerate(PLANE):

            @pl.when(inside(-b, -c))
            def _(s=s):
                plane_copy(j, s).wait_recv()

    def accumulate(width, base, messages, store):
        per_row = width // BLOCK

        def step(t, carry):
            rows = pl.ds(pl.multiple_of(t // per_row * TILE, TILE), TILE)
            cols = pl.ds(pl.multiple_of(t % per_row * BLOCK, BLOCK), BLOCK)
            sums = [base(k, rows, cols) for k in range(blocks)]
            for read, weight in messages:
                value = read(rows, cols).astype(jnp.float32)
                for k in range(blocks):
                    term = value * weight(k)
                    sums[k] = term if sums[k] is None else sums[k] + term
            for k in range(blocks):
                store(k, rows, cols, sums[k])
            return carry

        lax.fori_loop(0, BLOCK // TILE * per_row, step, 0)

    def from_recv(j, s, place):
        return lambda rows, cols: recvs[j][s, place, rows, cols]

    def own_weight(e):
        return lambda k: own_w[e * blocks + k]

    def totals(j, terms):
        def base(k, rows, cols):
            return pays[j][k, rows, cols].astype(jnp.float32)

        def store(k, rows, cols, value):
            tots[j][k, rows, cols] = value

        messages = []
        for a in terms:
            for s, (b, c) in enumerate(PLANE):
                messages.append((from_recv(j, s, a + 1), own_weight(number(a, b, c))))
            if a != 0:

                def read(rows, cols, a=a):
                    return parts[j][slot(a), maps[slot(a), 0, number(a, 0, 0)], rows, cols]

                messages.append((read, own_weight(number(a, 0, 0))))
        accumulate(widths[j], base, messages, store)

    stage(last, False)

    for a in shifts:
        map_copy(a).wait_recv()
        mover = pltpu.make_async_copy(map_in.at[slot(a)], maps.at[slot(a)], mapc_sem.at[slot(a)])
        mover.start()
        mover.wait()
    for a in (-1, 1):
        for b in (-1, 0, 1):
            for c in (-1, 0, 1):
                e = number(a, b, c)
                alive = inside(-b, -c)
                for k in range(blocks):
                    hit = (maps[slot(-a), 0, 25 - e] == k) & alive
                    relay_w[e * blocks + k] = jnp.where(hit, 1.0, 0.0).astype(jnp.float32)

    for a in shifts:
        for g in range(groups):
            x_copy(0, a, 2 * g, 2, g).wait_recv()
    stage(0, True)

    arrived(last)
    for target in shifts:
        messages = []
        for a in (-1, 1):
            if slot(a) != slot(target):
                continue
            for s, (b, c) in enumerate(PLANE):
                e = number(a, b, c)
                messages.append((from_recv(last, s, a + 1), lambda k, e=e: relay_w[e * blocks + k]))
            e = number(a, 0, 0)

            def read(rows, cols, e=e):
                return pays[last][map_ref[e], rows, cols]

            messages.append((read, lambda k, e=e: relay_w[e * blocks + k]))

        def store(k, rows, cols, value, target=target):
            comb[slot(target), k, rows, cols] = value.astype(jnp.bfloat16)

        accumulate(widths[last], lambda k, rows, cols: None, messages, store)
        b_copy(target).start()

    for j in range(1, last):
        for a in shifts:
            x_copy(j, a, 0, blocks, 0).wait_recv()
        stage(j, True)
    totals(last, (0,))

    counts = []
    for k in range(blocks):
        count = jnp.float32(1.0)
        for e in range(26):
            count = count + own_w[e * blocks + k]
        counts.append(count)

    stores = []

    def finish(j, start):
        lead = BLOCK if j == 0 else 0
        width = widths[j] - lead
        for k in range(blocks):
            summed = tots[j][k, :, lead:]
            if j == last:
                for a in shifts:
                    summed = summed + comb_in[slot(a), k].astype(jnp.float32)
            spot = pl.ds(k * BLOCK, BLOCK)
            value = jnp.dot(
                tots[0][k, :, :BLOCK],
                summed,
                precision=lax.Precision.HIGHEST,
                preferred_element_type=jnp.float32,
            )
            scaleds[j][spot, :] = (value / counts[k]).astype(jnp.bfloat16)
            asms[j][spot, :] = summed.astype(jnp.bfloat16)
        cols = pl.ds(start, width)
        out = pltpu.make_async_copy(asms[j], asm_hbm.at[:, cols], store_sem.at[0, j])
        out.start()
        stores.append(out)

        def step(t, carry):
            rows = pl.ds(pl.multiple_of(t * group_rows, group_rows), group_rows)
            upds[j][rows, :] = jnp.dot(
                schur[rows, :], scaleds[j][...], preferred_element_type=jnp.float32
            ).astype(jnp.bfloat16)
            return carry

        lax.fori_loop(0, groups, step, 0)
        out = pltpu.make_async_copy(upds[j], upd_hbm.at[:, cols], store_sem.at[1, j])
        out.start()
        stores.append(out)
        return start + width

    start = 0
    for j in range(last):
        arrived(j)
        totals(j, (-1, 0, 1))
        start = finish(j, start)
    for a in shifts:
        b_copy(a).wait_recv()
    finish(last, start)

    for a in shifts:
        map_copy(a).wait_send()
        for g in range(groups):
            x_copy(0, a, 2 * g, 2, g).wait_send()
        for j in range(1, last):
            x_copy(j, a, 0, blocks, 0).wait_send()
        b_copy(a).wait_send()
    for s, (b, c) in enumerate(PLANE):

        @pl.when(inside(b, c))
        def _(s=s):
            for j in range(last + 1):
                plane_copy(j, s).wait_send()

    for out in stores:
        out.wait()


def local(sizes, schur, block_map, vectors):
    matrix = schur[0, 0, 0]
    right_side = vectors[0, 0, 0]
    links = block_map[0, 0, 0]
    order, rhs = right_side.shape
    blocks = order // BLOCK
    groups = order // (2 * BLOCK)
    bf16, f32, i32 = jnp.bfloat16, jnp.float32, jnp.int32
    widths = (2 * BLOCK, rhs // 2 - BLOCK, rhs // 2)
    chunks = len(widths)
    near = 1 if sizes[0] == 2 else 2
    clean = (widths[0] - BLOCK,) + widths[1:]
    vmem, dma = pltpu.VMEM, pltpu.SemaphoreType.DMA
    scratch = [
        vmem((order, order), bf16),
        vmem((order, rhs), bf16),
        pltpu.SMEM((26 * blocks,), f32),
        pltpu.SMEM((26 * blocks,), f32),
        pltpu.SMEM((near, 8, 128), i32),
        vmem((8, 128), i32),
        vmem((near, 8, 128), i32),
        [vmem((blocks, BLOCK, w), bf16) for w in widths],
        [vmem((near, blocks, BLOCK, w), bf16) for w in widths[:-1]],
        [vmem((8, 3, BLOCK, w), bf16) for w in widths],
        [vmem((8, 3, BLOCK, w), bf16) for w in widths],
        vmem((near, blocks, BLOCK, widths[-1]), bf16),
        vmem((near, blocks, BLOCK, widths[-1]), bf16),
        [vmem((blocks, BLOCK, w), f32) for w in widths],
        [vmem((order, w), bf16) for w in clean],
        [vmem((order, w), bf16) for w in clean],
        [vmem((order, w), bf16) for w in clean],
        dma((groups + 1,)),
        dma((2, chunks)),
        dma((near,)),
        dma((near,)),
        dma((near,)),
        dma((chunks - 1, near, groups)),
        dma((chunks - 1, near, groups)),
        dma((chunks, 8)),
        dma((chunks, 8)),
        dma((near,)),
        dma((near,)),
    ]
    anywhere = pl.BlockSpec(memory_space=pl.ANY)
    assembled, update = pl.pallas_call(
        functools.partial(kernel, sizes, widths),
        out_shape=[jax.ShapeDtypeStruct((order, rhs), bf16)] * 2,
        in_specs=[pl.BlockSpec(memory_space=pltpu.SMEM), anywhere, anywhere],
        out_specs=[anywhere, anywhere],
        scratch_shapes=scratch,
        compiler_params=pltpu.CompilerParams(
            collective_id=0, has_side_effects=True, vmem_limit_bytes=60 * 1024 * 1024
        ),
    )(links, matrix, right_side)
    return assembled[None, None, None], update[None, None, None]


def solution(mesh):
    placed = (
        P("gx", "gy", "gz", None, None),
        P("gx", "gy", "gz", None),
        P("gx", "gy", "gz", None, None),
    )
    sizes = tuple(mesh.shape[name] for name in ("gx", "gy", "gz"))
    return jax.shard_map(
        functools.partial(local, sizes),
        mesh=mesh,
        in_specs=placed,
        out_specs=(P("gx", "gy", "gz", None, None), P("gx", "gy", "gz", None, None)),
        check_vma=False,
    )
```

```python
import functools

import jax
import jax.numpy as jnp
from jax import lax
from jax.experimental import pallas as pl
from jax.experimental.pallas import tpu as pltpu
from jax.sharding import PartitionSpec as P

BLOCK = 128
TILE = 32
MESH = pl.DeviceIdType.MESH
DIRS = [
    (a, b, c)
    for a in (-1, 0, 1)
    for b in (-1, 0, 1)
    for c in (-1, 0, 1)
    if (a, b, c) != (0, 0, 0)
]
PLANE = [(b, c) for b in (-1, 0, 1) for c in (-1, 0, 1) if (b, c) != (0, 0)]


def number(a, b, c):
    return DIRS.index((a, b, c))


def kernel(
    sizes,
    widths,
    starts,
    map_ref,
    schur_hbm,
    vec_hbm,
    asm_hbm,
    upd_hbm,
    schur,
    vec,
    own_w,
    relay_w,
    maps,
    map_out,
    map_in,
    pays,
    parts,
    stages,
    recvs,
    comb,
    comb_in,
    tots,
    coupling,
    scaleds,
    asms,
    upds,
    tile_sem,
    load_sem,
    store_sem,
    mapc_sem,
    map_send,
    map_recv,
    x_send,
    x_recv,
    p_send,
    p_recv,
    b_send,
    b_recv,
):
    gx, gy, gz = sizes
    order = schur.shape[0]
    blocks = order // BLOCK
    group_rows = 2 * BLOCK
    groups = order // group_rows
    far = (3, 4)
    p, q, r = lax.axis_index("gx"), lax.axis_index("gy"), lax.axis_index("gz")
    shifts = (1,) if gx == 2 else (-1, 1)

    def slot(a):
        return 0 if gx == 2 or a == -1 else 1

    def inside(b, c):
        return (q + b >= 0) & (q + b < gy) & (r + c >= 0) & (r + c < gz)

    def across(a):
        return {"gx": lax.rem(p + a + gx, gx), "gy": q, "gz": r}

    def beside(b, c):
        return {"gx": p, "gy": q + b, "gz": r + c}

    barrier = pltpu.get_barrier_semaphore()
    for a in shifts:
        pl.semaphore_signal(barrier, inc=1, device_id=across(a), device_id_type=MESH)
    for b, c in PLANE:

        @pl.when(inside(b, c))
        def _(b=b, c=c):
            pl.semaphore_signal(barrier, inc=1, device_id=beside(b, c), device_id_type=MESH)

    rows_near = 3 - jnp.where(q == 0, 1, 0) - jnp.where(q == gy - 1, 1, 0)
    cols_near = 3 - jnp.where(r == 0, 1, 0) - jnp.where(r == gz - 1, 1, 0)
    peers = rows_near * cols_near - 1 + len(shifts)

    tiles = []
    for k in range(blocks):
        spot = pl.ds(k * BLOCK, BLOCK)
        tile = pltpu.make_async_copy(schur_hbm.at[spot, spot], pays[0].at[k], tile_sem.at[k])
        tile.start()
        tiles.append(tile)
    vec_copy = pltpu.make_async_copy(vec_hbm, vec, load_sem.at[groups])
    vec_copy.start()
    loads = []
    for g in range(groups):
        rows = pl.ds(g * group_rows, group_rows)
        load = pltpu.make_async_copy(schur_hbm.at[rows], schur.at[rows], load_sem.at[g])
        load.start()
        loads.append(load)

    lanes = lax.broadcasted_iota(jnp.int32, (8, 128), 1)
    row = jnp.zeros((8, 128), jnp.int32)
    for e in range(26):
        row = jnp.where(lanes == e, map_ref[e], row)
    map_out[...] = row

    for e, (a, b, c) in enumerate(DIRS):
        alive = inside(-b, -c)
        for k in range(blocks):
            hit = (map_ref[25 - e] == k) & alive
            own_w[e * blocks + k] = jnp.where(hit, 1.0, 0.0).astype(jnp.float32)
    for s, (b, c) in enumerate(PLANE):

        @pl.when(jnp.logical_not(inside(-b, -c)))
        def _(s=s):
            for recv in recvs:
                recv[s] = jnp.zeros(recv.shape[1:], recv.dtype)

    def x_copy(j, a, lo, n, sem):
        return pltpu.make_async_remote_copy(
            src_ref=pays[j].at[pl.ds(lo, n)],
            dst_ref=parts[j].at[slot(a), pl.ds(lo, n)],
            send_sem=x_send.at[j, slot(a), sem],
            recv_sem=x_recv.at[j, slot(a), sem],
            device_id=across(a),
            device_id_type=MESH,
        )

    def map_copy(a):
        return pltpu.make_async_remote_copy(
            src_ref=map_out,
            dst_ref=map_in.at[slot(a)],
            send_sem=map_send.at[slot(a)],
            recv_sem=map_recv.at[slot(a)],
            device_id=across(a),
            device_id_type=MESH,
        )

    def plane_copy(j, s):
        b, c = PLANE[s]
        return pltpu.make_async_remote_copy(
            src_ref=stages[j].at[s],
            dst_ref=recvs[j].at[s],
            send_sem=p_send.at[j, s],
            recv_sem=p_recv.at[j, s],
            device_id=beside(b, c),
            device_id_type=MESH,
        )

    def b_copy(i, a):
        return pltpu.make_async_remote_copy(
            src_ref=comb.at[i, slot(a)],
            dst_ref=comb_in.at[i, slot(a)],
            send_sem=b_send.at[i, slot(a)],
            recv_sem=b_recv.at[i, slot(a)],
            device_id=across(a),
            device_id_type=MESH,
        )

    for tile in tiles:
        tile.wait()
    pl.semaphore_wait(barrier, peers)
    for a in shifts:
        map_copy(a).start()
        x_copy(0, a, 0, blocks, 0).start()

    vec_copy.wait()
    for g in range(groups):
        loads[g].wait()
        rows = pl.ds(g * group_rows, group_rows)
        product = jnp.dot(schur[rows, :], vec[...], preferred_element_type=jnp.float32)
        product = product.astype(jnp.bfloat16)
        for half in range(2):
            for j in range(1, len(widths)):
                pays[j][2 * g + half] = product[
                    half * BLOCK : (half + 1) * BLOCK, starts[j] : starts[j] + widths[j]
                ]
        for a in shifts:
            x_copy(1, a, 2 * g, 2, g).start()
    for a in shifts:
        x_copy(2, a, 0, blocks, 0).start()

    def stage(j, near):
        for s, (b, c) in enumerate(PLANE):

            @pl.when(inside(b, c))
            def _(s=s, b=b, c=c):
                stages[j][s, 1] = pays[j][map_ref[number(0, b, c)]]
                for place, a in ((0, -1), (2, 1)):
                    if near:
                        stages[j][s, place] = parts[j][
                            slot(a), maps[slot(a), 0, number(a, b, c)]
                        ]
                    else:
                        stages[j][s, place] = pays[j][map_ref[number(a, b, c)]]
                plane_copy(j, s).start()

    def arrived(j):
        for s, (b, c) in enumerate(PLANE):

            @pl.when(inside(-b, -c))
            def _(s=s):
                plane_copy(j, s).wait_recv()

    def accumulate(width, base, messages, store):
        per_row = width // BLOCK

        def step(t, carry):
            rows = pl.ds(pl.multiple_of(t // per_row * TILE, TILE), TILE)
            cols = pl.ds(pl.multiple_of(t % per_row * BLOCK, BLOCK), BLOCK)
            sums = [base(k, rows, cols) for k in range(blocks)]
            for read, weight in messages:
                value = read(rows, cols).astype(jnp.float32)
                for k in range(blocks):
                    term = value * weight(k)
                    sums[k] = term if sums[k] is None else sums[k] + term
            for k in range(blocks):
                store(k, rows, cols, sums[k])
            return carry

        lax.fori_loop(0, BLOCK // TILE * per_row, step, 0)

    def from_recv(j, s, place):
        return lambda rows, cols: recvs[j][s, place, rows, cols]

    def own_weight(e):
        return lambda k: own_w[e * blocks + k]

    def totals(j, terms):
        def base(k, rows, cols):
            return pays[j][k, rows, cols].astype(jnp.float32)

        def store(k, rows, cols, value):
            tots[j][k, rows, cols] = value

        messages = []
        for a in terms:
            for s, (b, c) in enumerate(PLANE):
                messages.append((from_recv(j, s, a + 1), own_weight(number(a, b, c))))
            if a != 0:

                def read(rows, cols, a=a):
                    return parts[j][slot(a), maps[slot(a), 0, number(a, 0, 0)], rows, cols]

                messages.append((read, own_weight(number(a, 0, 0))))
        accumulate(widths[j], base, messages, store)

    for j in far:
        stage(j, False)

    for a in shifts:
        map_copy(a).wait_recv()
        mover = pltpu.make_async_copy(map_in.at[slot(a)], maps.at[slot(a)], mapc_sem.at[slot(a)])
        mover.start()
        mover.wait()
    for a in (-1, 1):
        for b in (-1, 0, 1):
            for c in (-1, 0, 1):
                e = number(a, b, c)
                alive = inside(-b, -c)
                for k in range(blocks):
                    hit = (maps[slot(-a), 0, 25 - e] == k) & alive
                    relay_w[e * blocks + k] = jnp.where(hit, 1.0, 0.0).astype(jnp.float32)

    def relay(j):
        i = far.index(j)
        arrived(j)
        for target in shifts:
            messages = []
            for a in (-1, 1):
                if slot(a) != slot(target):
                    continue
                for s, (b, c) in enumerate(PLANE):
                    e = number(a, b, c)
                    messages.append(
                        (from_recv(j, s, a + 1), lambda k, e=e: relay_w[e * blocks + k])
                    )
                e = number(a, 0, 0)

                def read(rows, cols, e=e):
                    return pays[j][map_ref[e], rows, cols]

                messages.append((read, lambda k, e=e: relay_w[e * blocks + k]))

            def store(k, rows, cols, value, target=target):
                comb[i, slot(target), k, rows, cols] = value.astype(jnp.bfloat16)

            accumulate(widths[j], lambda k, rows, cols: None, messages, store)
            b_copy(i, target).start()

    for a in shifts:
        x_copy(0, a, 0, blocks, 0).wait_recv()
    stage(0, True)
    relay(far[0])
    for a in shifts:
        for g in range(groups):
            x_copy(1, a, 2 * g, 2, g).wait_recv()
    stage(1, True)
    relay(far[1])
    totals(far[0], (0,))
    for a in shifts:
        x_copy(2, a, 0, blocks, 0).wait_recv()
    stage(2, True)
    totals(far[1], (0,))

    counts = []
    for k in range(blocks):
        count = jnp.float32(1.0)
        for e in range(26):
            count = count + own_w[e * blocks + k]
        counts.append(count)

    def split(value):
        high = value.astype(jnp.bfloat16)
        low = (value - high.astype(jnp.float32)).astype(jnp.bfloat16)
        return high, low

    arrived(0)
    totals(0, (-1, 0, 1))
    for k in range(blocks):
        high, low = split(tots[0][k])
        coupling[k, :, :BLOCK] = high
        coupling[k, :, BLOCK:] = low

    stores = []
    for i, (j, jj) in enumerate(((1, far[0]), (2, far[1]))):
        arrived(j)
        totals(j, (-1, 0, 1))
        for a in shifts:
            b_copy(i, a).wait_recv()
        width = widths[j]
        for k in range(blocks):
            far_sum = tots[jj][k]
            for a in shifts:
                far_sum = far_sum + comb_in[i, slot(a), k].astype(jnp.float32)
            summed = jnp.concatenate([tots[j][k], far_sum], axis=1)
            high, low = split(summed)
            spot = pl.ds(k * BLOCK, BLOCK)
            value = jnp.dot(
                coupling[k],
                jnp.concatenate([high, high], axis=0),
                preferred_element_type=jnp.float32,
            ) + jnp.dot(
                coupling[k],
                jnp.concatenate([low, low], axis=0),
                preferred_element_type=jnp.float32,
            )
            scaleds[i][spot, :] = (value / counts[k]).astype(jnp.bfloat16)
            asms[i][spot, :] = high
        cols = pl.ds(starts[j], 2 * width)
        out = pltpu.make_async_copy(asms[i], asm_hbm.at[:, cols], store_sem.at[0, i])
        out.start()
        stores.append(out)

        def step(t, carry, i=i):
            rows = pl.ds(pl.multiple_of(t * group_rows, group_rows), group_rows)
            upds[i][rows, :] = jnp.dot(
                schur[rows, :], scaleds[i][...], preferred_element_type=jnp.float32
            ).astype(jnp.bfloat16)
            return carry

        lax.fori_loop(0, groups, step, 0)
        out = pltpu.make_async_copy(upds[i], upd_hbm.at[:, cols], store_sem.at[1, i])
        out.start()
        stores.append(out)

    for a in shifts:
        map_copy(a).wait_send()
        x_copy(0, a, 0, blocks, 0).wait_send()
        for g in range(groups):
            x_copy(1, a, 2 * g, 2, g).wait_send()
        x_copy(2, a, 0, blocks, 0).wait_send()
        for i in range(2):
            b_copy(i, a).wait_send()
    for s, (b, c) in enumerate(PLANE):

        @pl.when(inside(b, c))
        def _(s=s):
            for j in range(len(widths)):
                plane_copy(j, s).wait_send()

    for out in stores:
        out.wait()


def local(sizes, schur, block_map, vectors):
    matrix = schur[0, 0, 0]
    right_side = vectors[0, 0, 0]
    links = block_map[0, 0, 0]
    order, rhs = right_side.shape
    blocks = order // BLOCK
    groups = order // (2 * BLOCK)
    bf16, f32, i32 = jnp.bfloat16, jnp.float32, jnp.int32
    share = rhs // 4
    widths = (BLOCK, share, share, share, share)
    starts = (0, 0, 2 * share, share, 3 * share)
    chunks = len(widths)
    near = 1 if sizes[0] == 2 else 2
    vmem, dma = pltpu.VMEM, pltpu.SemaphoreType.DMA
    scratch = [
        vmem((order, order), bf16),
        vmem((order, rhs), bf16),
        pltpu.SMEM((26 * blocks,), f32),
        pltpu.SMEM((26 * blocks,), f32),
        pltpu.SMEM((near, 8, 128), i32),
        vmem((8, 128), i32),
        vmem((near, 8, 128), i32),
        [vmem((blocks, BLOCK, w), bf16) for w in widths],
        [vmem((near, blocks, BLOCK, w), bf16) for w in widths[:3]],
        [vmem((8, 3, BLOCK, w), bf16) for w in widths],
        [vmem((8, 3, BLOCK, w), bf16) for w in widths],
        vmem((2, near, blocks, BLOCK, share), bf16),
        vmem((2, near, blocks, BLOCK, share), bf16),
        [vmem((blocks, BLOCK, w), f32) for w in widths],
        vmem((blocks, BLOCK, 2 * BLOCK), bf16),
        [vmem((order, 2 * share), bf16) for _ in range(2)],
        [vmem((order, 2 * share), bf16) for _ in range(2)],
        [vmem((order, 2 * share), bf16) for _ in range(2)],
        dma((blocks,)),
        dma((groups + 1,)),
        dma((2, 2)),
        dma((near,)),
        dma((near,)),
        dma((near,)),
        dma((3, near, groups)),
        dma((3, near, groups)),
        dma((chunks, 8)),
        dma((chunks, 8)),
        dma((2, near)),
        dma((2, near)),
    ]
    anywhere = pl.BlockSpec(memory_space=pl.ANY)
    assembled, update = pl.pallas_call(
        functools.partial(kernel, sizes, widths, starts),
        out_shape=[jax.ShapeDtypeStruct((order, rhs), bf16)] * 2,
        in_specs=[pl.BlockSpec(memory_space=pltpu.SMEM), anywhere, anywhere],
        out_specs=[anywhere, anywhere],
        scratch_shapes=scratch,
        compiler_params=pltpu.CompilerParams(
            collective_id=0, has_side_effects=True, vmem_limit_bytes=60 * 1024 * 1024
        ),
    )(links, matrix, right_side)
    return assembled[None, None, None], update[None, None, None]


def solution(mesh):
    placed = (
        P("gx", "gy", "gz", None, None),
        P("gx", "gy", "gz", None),
        P("gx", "gy", "gz", None, None),
    )
    sizes = tuple(mesh.shape[name] for name in ("gx", "gy", "gz"))
    return jax.shard_map(
        functools.partial(local, sizes),
        mesh=mesh,
        in_specs=placed,
        out_specs=(P("gx", "gy", "gz", None, None), P("gx", "gy", "gz", None, None)),
        check_vma=False,
    )
```

```python
import functools

import jax
import jax.numpy as jnp
from jax import lax
from jax.experimental import pallas as pl
from jax.experimental.pallas import tpu as pltpu
from jax.sharding import PartitionSpec as P

BLOCK = 128
TILE = 32
MESH = pl.DeviceIdType.MESH
DIRS = [
    (a, b, c)
    for a in (-1, 0, 1)
    for b in (-1, 0, 1)
    for c in (-1, 0, 1)
    if (a, b, c) != (0, 0, 0)
]
PLANE = [(b, c) for b in (-1, 0, 1) for c in (-1, 0, 1) if (b, c) != (0, 0)]


def number(a, b, c):
    return DIRS.index((a, b, c))


def kernel(
    sizes,
    widths,
    starts,
    map_ref,
    schur_hbm,
    vec_hbm,
    asm_hbm,
    upd_hbm,
    schur,
    vec,
    own_w,
    relay_w,
    maps,
    map_out,
    map_in,
    pays,
    parts,
    stages,
    recvs,
    comb,
    comb_in,
    tots,
    coupling,
    scaleds,
    asms,
    upds,
    tile_sem,
    load_sem,
    store_sem,
    mapc_sem,
    map_send,
    map_recv,
    x_send,
    x_recv,
    p_send,
    p_recv,
    b_send,
    b_recv,
):
    gx, gy, gz = sizes
    order = schur.shape[0]
    blocks = order // BLOCK
    group_rows = 2 * BLOCK
    groups = order // group_rows
    far = (3, 4)
    p, q, r = lax.axis_index("gx"), lax.axis_index("gy"), lax.axis_index("gz")
    shifts = (1,) if gx == 2 else (-1, 1)

    def slot(a):
        return 0 if gx == 2 or a == -1 else 1

    def inside(b, c):
        return (q + b >= 0) & (q + b < gy) & (r + c >= 0) & (r + c < gz)

    def across(a):
        return {"gx": lax.rem(p + a + gx, gx), "gy": q, "gz": r}

    def beside(b, c):
        return {"gx": p, "gy": q + b, "gz": r + c}

    barrier = pltpu.get_barrier_semaphore()
    for a in shifts:
        pl.semaphore_signal(barrier, inc=1, device_id=across(a), device_id_type=MESH)
    for b, c in PLANE:

        @pl.when(inside(b, c))
        def _(b=b, c=c):
            pl.semaphore_signal(barrier, inc=1, device_id=beside(b, c), device_id_type=MESH)

    rows_near = 3 - jnp.where(q == 0, 1, 0) - jnp.where(q == gy - 1, 1, 0)
    cols_near = 3 - jnp.where(r == 0, 1, 0) - jnp.where(r == gz - 1, 1, 0)
    peers = rows_near * cols_near - 1 + len(shifts)

    tiles = []
    for k in range(blocks):
        spot = pl.ds(k * BLOCK, BLOCK)
        tile = pltpu.make_async_copy(schur_hbm.at[spot, spot], pays[0].at[k], tile_sem.at[k])
        tile.start()
        tiles.append(tile)
    vec_copy = pltpu.make_async_copy(vec_hbm, vec, load_sem.at[groups])
    vec_copy.start()
    loads = []
    for g in range(groups):
        rows = pl.ds(g * group_rows, group_rows)
        load = pltpu.make_async_copy(schur_hbm.at[rows], schur.at[rows], load_sem.at[g])
        load.start()
        loads.append(load)

    lanes = lax.broadcasted_iota(jnp.int32, (8, 128), 1)
    row = jnp.zeros((8, 128), jnp.int32)
    for e in range(26):
        row = jnp.where(lanes == e, map_ref[e], row)
    map_out[...] = row

    for e, (a, b, c) in enumerate(DIRS):
        alive = inside(-b, -c)
        for k in range(blocks):
            hit = (map_ref[25 - e] == k) & alive
            own_w[e * blocks + k] = jnp.where(hit, 1.0, 0.0).astype(jnp.float32)
    for s, (b, c) in enumerate(PLANE):

        @pl.when(jnp.logical_not(inside(-b, -c)))
        def _(s=s):
            for recv in recvs:
                recv[s] = jnp.zeros(recv.shape[1:], recv.dtype)

    def x_copy(j, a, lo, n, sem):
        return pltpu.make_async_remote_copy(
            src_ref=pays[j].at[pl.ds(lo, n)],
            dst_ref=parts[j].at[slot(a), pl.ds(lo, n)],
            send_sem=x_send.at[j, slot(a), sem],
            recv_sem=x_recv.at[j, slot(a), sem],
            device_id=across(a),
            device_id_type=MESH,
        )

    def map_copy(a):
        return pltpu.make_async_remote_copy(
            src_ref=map_out,
            dst_ref=map_in.at[slot(a)],
            send_sem=map_send.at[slot(a)],
            recv_sem=map_recv.at[slot(a)],
            device_id=across(a),
            device_id_type=MESH,
        )

    def plane_copy(j, s):
        b, c = PLANE[s]
        return pltpu.make_async_remote_copy(
            src_ref=stages[j].at[s],
            dst_ref=recvs[j].at[s],
            send_sem=p_send.at[j, s],
            recv_sem=p_recv.at[j, s],
            device_id=beside(b, c),
            device_id_type=MESH,
        )

    def b_copy(i, a):
        return pltpu.make_async_remote_copy(
            src_ref=comb.at[i, slot(a)],
            dst_ref=comb_in.at[i, slot(a)],
            send_sem=b_send.at[i, slot(a)],
            recv_sem=b_recv.at[i, slot(a)],
            device_id=across(a),
            device_id_type=MESH,
        )

    for tile in tiles:
        tile.wait()
    pl.semaphore_wait(barrier, peers)
    for a in shifts:
        map_copy(a).start()
        x_copy(0, a, 0, blocks, 0).start()

    vec_copy.wait()
    for g in range(groups):
        loads[g].wait()
        rows = pl.ds(g * group_rows, group_rows)
        product = jnp.dot(schur[rows, :], vec[...], preferred_element_type=jnp.float32)
        product = product.astype(jnp.bfloat16)
        for half in range(2):
            for j in range(1, len(widths)):
                pays[j][2 * g + half] = product[
                    half * BLOCK : (half + 1) * BLOCK, starts[j] : starts[j] + widths[j]
                ]
        for a in shifts:
            x_copy(1, a, 2 * g, 2, g).start()
    for a in shifts:
        x_copy(2, a, 0, blocks, 0).start()

    def stage(j, near):
        for s, (b, c) in enumerate(PLANE):

            @pl.when(inside(b, c))
            def _(s=s, b=b, c=c):
                stages[j][s, 1] = pays[j][map_ref[number(0, b, c)]]
                for place, a in ((0, -1), (2, 1)):
                    if near:
                        stages[j][s, place] = parts[j][
                            slot(a), maps[slot(a), 0, number(a, b, c)]
                        ]
                    else:
                        stages[j][s, place] = pays[j][map_ref[number(a, b, c)]]
                plane_copy(j, s).start()

    def arrived(j):
        for s, (b, c) in enumerate(PLANE):

            @pl.when(inside(-b, -c))
            def _(s=s):
                plane_copy(j, s).wait_recv()

    def accumulate(width, base, messages, store):
        per_row = width // BLOCK

        def step(t, carry):
            rows = pl.ds(pl.multiple_of(t // per_row * TILE, TILE), TILE)
            cols = pl.ds(pl.multiple_of(t % per_row * BLOCK, BLOCK), BLOCK)
            sums = [base(k, rows, cols) for k in range(blocks)]
            for read, weight in messages:
                value = read(rows, cols).astype(jnp.float32)
                for k in range(blocks):
                    term = value * weight(k)
                    sums[k] = term if sums[k] is None else sums[k] + term
            for k in range(blocks):
                store(k, rows, cols, sums[k])
            return carry

        lax.fori_loop(0, BLOCK // TILE * per_row, step, 0)

    def from_recv(j, s, place):
        return lambda rows, cols: recvs[j][s, place, rows, cols]

    def own_weight(e):
        return lambda k: own_w[e * blocks + k]

    def totals(j, terms):
        def base(k, rows, cols):
            return pays[j][k, rows, cols].astype(jnp.float32)

        def store(k, rows, cols, value):
            tots[j][k, rows, cols] = value

        messages = []
        for a in terms:
            for s, (b, c) in enumerate(PLANE):
                messages.append((from_recv(j, s, a + 1), own_weight(number(a, b, c))))
            if a != 0:

                def read(rows, cols, a=a):
                    return parts[j][slot(a), maps[slot(a), 0, number(a, 0, 0)], rows, cols]

                messages.append((read, own_weight(number(a, 0, 0))))
        accumulate(widths[j], base, messages, store)

    for j in far:
        stage(j, False)

    for a in shifts:
        map_copy(a).wait_recv()
        mover = pltpu.make_async_copy(map_in.at[slot(a)], maps.at[slot(a)], mapc_sem.at[slot(a)])
        mover.start()
        mover.wait()
    for a in (-1, 1):
        for b in (-1, 0, 1):
            for c in (-1, 0, 1):
                e = number(a, b, c)
                alive = inside(-b, -c)
                for k in range(blocks):
                    hit = (maps[slot(-a), 0, 25 - e] == k) & alive
                    relay_w[e * blocks + k] = jnp.where(hit, 1.0, 0.0).astype(jnp.float32)

    def relay(j):
        i = far.index(j)
        arrived(j)
        for target in shifts:
            messages = []
            for a in (-1, 1):
                if slot(a) != slot(target):
                    continue
                for s, (b, c) in enumerate(PLANE):
                    e = number(a, b, c)
                    messages.append(
                        (from_recv(j, s, a + 1), lambda k, e=e: relay_w[e * blocks + k])
                    )
                e = number(a, 0, 0)

                def read(rows, cols, e=e):
                    return pays[j][map_ref[e], rows, cols]

                messages.append((read, lambda k, e=e: relay_w[e * blocks + k]))

            def store(k, rows, cols, value, target=target):
                comb[i, slot(target), k, rows, cols] = value.astype(jnp.bfloat16)

            accumulate(widths[j], lambda k, rows, cols: None, messages, store)
            b_copy(i, target).start()

    for a in shifts:
        x_copy(0, a, 0, blocks, 0).wait_recv()
    stage(0, True)
    relay(far[0])
    for a in shifts:
        for g in range(groups):
            x_copy(1, a, 2 * g, 2, g).wait_recv()
    stage(1, True)
    relay(far[1])
    totals(far[0], (0,))
    for a in shifts:
        x_copy(2, a, 0, blocks, 0).wait_recv()
    stage(2, True)
    totals(far[1], (0,))

    counts = []
    for k in range(blocks):
        count = jnp.float32(1.0)
        for e in range(26):
            count = count + own_w[e * blocks + k]
        counts.append(count)

    def split(value):
        high = value.astype(jnp.bfloat16)
        low = (value - high.astype(jnp.float32)).astype(jnp.bfloat16)
        return high, low

    arrived(0)
    totals(0, (-1, 0, 1))
    for k in range(blocks):
        high, low = split(tots[0][k])
        coupling[k, :, :BLOCK] = high
        coupling[k, :, BLOCK:] = low

    stores = []
    for i, (j, jj) in enumerate(((1, far[0]), (2, far[1]))):
        arrived(j)
        totals(j, (-1, 0, 1))
        for a in shifts:
            b_copy(i, a).wait_recv()
        width = widths[j]
        for k in range(blocks):
            far_sum = tots[jj][k]
            for a in shifts:
                far_sum = far_sum + comb_in[i, slot(a), k].astype(jnp.float32)
            summed = jnp.concatenate([tots[j][k], far_sum], axis=1)
            high, low = split(summed)
            spot = pl.ds(k * BLOCK, BLOCK)
            value = jnp.dot(
                coupling[k],
                jnp.concatenate([high, high], axis=0),
                preferred_element_type=jnp.float32,
            ) + jnp.dot(
                coupling[k],
                jnp.concatenate([low, low], axis=0),
                preferred_element_type=jnp.float32,
            )
            scaleds[i][spot, :] = (value / counts[k]).astype(jnp.bfloat16)
            asms[i][spot, :] = high
        cols = pl.ds(starts[j], 2 * width)
        out = pltpu.make_async_copy(asms[i], asm_hbm.at[:, cols], store_sem.at[0, i])
        out.start()
        stores.append(out)

        def step(t, carry, i=i):
            rows = pl.ds(pl.multiple_of(t * group_rows, group_rows), group_rows)
            upds[i][rows, :] = jnp.dot(
                schur[rows, :], scaleds[i][...], preferred_element_type=jnp.float32
            ).astype(jnp.bfloat16)
            return carry

        lax.fori_loop(0, groups, step, 0)
        out = pltpu.make_async_copy(upds[i], upd_hbm.at[:, cols], store_sem.at[1, i])
        out.start()
        stores.append(out)

    for a in shifts:
        map_copy(a).wait_send()
        x_copy(0, a, 0, blocks, 0).wait_send()
        for g in range(groups):
            x_copy(1, a, 2 * g, 2, g).wait_send()
        x_copy(2, a, 0, blocks, 0).wait_send()
        for i in range(2):
            b_copy(i, a).wait_send()
    for s, (b, c) in enumerate(PLANE):

        @pl.when(inside(b, c))
        def _(s=s):
            for j in range(len(widths)):
                plane_copy(j, s).wait_send()

    for out in stores:
        out.wait()


def local(sizes, schur, block_map, vectors):
    matrix = schur[0, 0, 0]
    right_side = vectors[0, 0, 0]
    links = block_map[0, 0, 0]
    order, rhs = right_side.shape
    blocks = order // BLOCK
    groups = order // (2 * BLOCK)
    bf16, f32, i32 = jnp.bfloat16, jnp.float32, jnp.int32
    share = rhs // 4
    widths = (BLOCK, share, share, share, share)
    starts = (0, 0, 2 * share, share, 3 * share)
    chunks = len(widths)
    near = 1 if sizes[0] == 2 else 2
    vmem, dma = pltpu.VMEM, pltpu.SemaphoreType.DMA
    scratch = [
        vmem((order, order), bf16),
        vmem((order, rhs), bf16),
        pltpu.SMEM((26 * blocks,), f32),
        pltpu.SMEM((26 * blocks,), f32),
        pltpu.SMEM((near, 8, 128), i32),
        vmem((8, 128), i32),
        vmem((near, 8, 128), i32),
        [vmem((blocks, BLOCK, w), bf16) for w in widths],
        [vmem((near, blocks, BLOCK, w), bf16) for w in widths[:3]],
        [vmem((8, 3, BLOCK, w), bf16) for w in widths],
        [vmem((8, 3, BLOCK, w), bf16) for w in widths],
        vmem((2, near, blocks, BLOCK, share), bf16),
        vmem((2, near, blocks, BLOCK, share), bf16),
        [vmem((blocks, BLOCK, w), f32) for w in widths],
        vmem((blocks, BLOCK, 2 * BLOCK), bf16),
        [vmem((order, 2 * share), bf16) for _ in range(2)],
        [vmem((order, 2 * share), bf16) for _ in range(2)],
        [vmem((order, 2 * share), bf16) for _ in range(2)],
        dma((blocks,)),
        dma((groups + 1,)),
        dma((2, 2)),
        dma((near,)),
        dma((near,)),
        dma((near,)),
        dma((3, near, groups)),
        dma((3, near, groups)),
        dma((chunks, 8)),
        dma((chunks, 8)),
        dma((2, near)),
        dma((2, near)),
    ]
    anywhere = pl.BlockSpec(memory_space=pl.ANY)
    assembled, update = pl.pallas_call(
        functools.partial(kernel, sizes, widths, starts),
        out_shape=[jax.ShapeDtypeStruct((order, rhs), bf16)] * 2,
        in_specs=[pl.BlockSpec(memory_space=pltpu.SMEM), anywhere, anywhere],
        out_specs=[anywhere, anywhere],
        scratch_shapes=scratch,
        compiler_params=pltpu.CompilerParams(
            collective_id=0, has_side_effects=True, vmem_limit_bytes=51 * 1024 * 1024
        ),
    )(links, matrix, right_side)
    return assembled[None, None, None], update[None, None, None]


def solution(mesh):
    placed = (
        P("gx", "gy", "gz", None, None),
        P("gx", "gy", "gz", None),
        P("gx", "gy", "gz", None, None),
    )
    sizes = tuple(mesh.shape[name] for name in ("gx", "gy", "gz"))
    return jax.shard_map(
        functools.partial(local, sizes),
        mesh=mesh,
        in_specs=placed,
        out_specs=(P("gx", "gy", "gz", None, None), P("gx", "gy", "gz", None, None)),
        check_vma=False,
    )
```

```python
import functools

import jax
import jax.numpy as jnp
from jax import lax
from jax.experimental import pallas as pl
from jax.experimental.pallas import tpu as pltpu
from jax.sharding import PartitionSpec as P

BLOCK = 128
TILE = 32
MESH = pl.DeviceIdType.MESH
DIRS = [
    (a, b, c)
    for a in (-1, 0, 1)
    for b in (-1, 0, 1)
    for c in (-1, 0, 1)
    if (a, b, c) != (0, 0, 0)
]
PLANE = [(b, c) for b in (-1, 0, 1) for c in (-1, 0, 1) if (b, c) != (0, 0)]


def number(a, b, c):
    return DIRS.index((a, b, c))


def kernel(
    sizes,
    widths,
    starts,
    map_ref,
    schur_hbm,
    vec_hbm,
    asm_hbm,
    upd_hbm,
    schur,
    vec,
    own_w,
    relay_w,
    maps,
    map_out,
    map_in,
    pays,
    parts,
    stages,
    recvs,
    comb,
    comb_in,
    tots,
    coupling,
    scaleds,
    asms,
    upds,
    tile_sem,
    load_sem,
    store_sem,
    mapc_sem,
    map_send,
    map_recv,
    x_send,
    x_recv,
    p_send,
    p_recv,
    b_send,
    b_recv,
):
    gx, gy, gz = sizes
    order = schur.shape[0]
    blocks = order // BLOCK
    group_rows = 2 * BLOCK
    groups = order // group_rows
    far = (3, 4)
    p, q, r = lax.axis_index("gx"), lax.axis_index("gy"), lax.axis_index("gz")
    shifts = (1,) if gx == 2 else (-1, 1)

    def slot(a):
        return 0 if gx == 2 or a == -1 else 1

    def inside(b, c):
        return (q + b >= 0) & (q + b < gy) & (r + c >= 0) & (r + c < gz)

    def across(a):
        return {"gx": lax.rem(p + a + gx, gx), "gy": q, "gz": r}

    def beside(b, c):
        return {"gx": p, "gy": q + b, "gz": r + c}

    barrier = pltpu.get_barrier_semaphore()
    for a in shifts:
        pl.semaphore_signal(barrier, inc=1, device_id=across(a), device_id_type=MESH)
    for b, c in PLANE:

        @pl.when(inside(b, c))
        def _(b=b, c=c):
            pl.semaphore_signal(barrier, inc=1, device_id=beside(b, c), device_id_type=MESH)

    rows_near = 3 - jnp.where(q == 0, 1, 0) - jnp.where(q == gy - 1, 1, 0)
    cols_near = 3 - jnp.where(r == 0, 1, 0) - jnp.where(r == gz - 1, 1, 0)
    peers = rows_near * cols_near - 1 + len(shifts)

    tiles = []
    for k in range(blocks):
        spot = pl.ds(k * BLOCK, BLOCK)
        tile = pltpu.make_async_copy(schur_hbm.at[spot, spot], pays[0].at[k], tile_sem.at[k])
        tile.start()
        tiles.append(tile)
    vec_copy = pltpu.make_async_copy(vec_hbm, vec, load_sem.at[groups])
    vec_copy.start()
    loads = []
    for g in range(groups):
        rows = pl.ds(g * group_rows, group_rows)
        load = pltpu.make_async_copy(schur_hbm.at[rows], schur.at[rows], load_sem.at[g])
        load.start()
        loads.append(load)

    def x_copy(j, a, lo, n, sem):
        return pltpu.make_async_remote_copy(
            src_ref=pays[j].at[pl.ds(lo, n)],
            dst_ref=parts[j].at[slot(a), pl.ds(lo, n)],
            send_sem=x_send.at[j, slot(a), sem],
            recv_sem=x_recv.at[j, slot(a), sem],
            device_id=across(a),
            device_id_type=MESH,
        )

    def map_copy(a):
        return pltpu.make_async_remote_copy(
            src_ref=map_out,
            dst_ref=map_in.at[slot(a)],
            send_sem=map_send.at[slot(a)],
            recv_sem=map_recv.at[slot(a)],
            device_id=across(a),
            device_id_type=MESH,
        )

    def plane_copy(j, s):
        b, c = PLANE[s]
        return pltpu.make_async_remote_copy(
            src_ref=stages[j].at[s],
            dst_ref=recvs[j].at[s],
            send_sem=p_send.at[j, s],
            recv_sem=p_recv.at[j, s],
            device_id=beside(b, c),
            device_id_type=MESH,
        )

    def b_copy(i, a):
        return pltpu.make_async_remote_copy(
            src_ref=comb.at[i, slot(a)],
            dst_ref=comb_in.at[i, slot(a)],
            send_sem=b_send.at[i, slot(a)],
            recv_sem=b_recv.at[i, slot(a)],
            device_id=across(a),
            device_id_type=MESH,
        )

    for tile in tiles:
        tile.wait()
    pl.semaphore_wait(barrier, peers)
    for a in shifts:
        x_copy(0, a, 0, blocks, 0).start()


    lanes = lax.broadcasted_iota(jnp.int32, (8, 128), 1)
    row = jnp.zeros((8, 128), jnp.int32)
    for e in range(26):
        row = jnp.where(lanes == e, map_ref[e], row)
    map_out[...] = row

    for a in shifts:
        map_copy(a).start()

    vec_copy.wait()
    for g in range(groups):
        loads[g].wait()
        rows = pl.ds(g * group_rows, group_rows)
        product = jnp.dot(schur[rows, :], vec[...], preferred_element_type=jnp.float32)
        product = product.astype(jnp.bfloat16)
        for half in range(2):
            for j in range(1, len(widths)):
                pays[j][2 * g + half] = product[
                    half * BLOCK : (half + 1) * BLOCK, starts[j] : starts[j] + widths[j]
                ]
        for a in shifts:
            x_copy(1, a, 2 * g, 2, g).start()
    for a in shifts:
        x_copy(2, a, 0, blocks, 0).start()

    def stage(j, near):
        for s, (b, c) in enumerate(PLANE):

            @pl.when(inside(b, c))
            def _(s=s, b=b, c=c):
                stages[j][s, 1] = pays[j][map_ref[number(0, b, c)]]
                for place, a in ((0, -1), (2, 1)):
                    if near:
                        stages[j][s, place] = parts[j][
                            slot(a), maps[slot(a), 0, number(a, b, c)]
                        ]
                    else:
                        stages[j][s, place] = pays[j][map_ref[number(a, b, c)]]
                plane_copy(j, s).start()

    def arrived(j, rows=(-1, 0, 1)):
        for s, (b, c) in enumerate(PLANE):
            if b not in rows:
                continue

            @pl.when(inside(-b, -c))
            def _(s=s):
                plane_copy(j, s).wait_recv()

    def accumulate(width, base, messages, store):
        per_row = width // BLOCK

        def step(t, carry):
            rows = pl.ds(pl.multiple_of(t // per_row * TILE, TILE), TILE)
            cols = pl.ds(pl.multiple_of(t % per_row * BLOCK, BLOCK), BLOCK)
            sums = [base(k, rows, cols) for k in range(blocks)]
            for read, weight in messages:
                value = read(rows, cols).astype(jnp.float32)
                for k in range(blocks):
                    term = value * weight(k)
                    sums[k] = term if sums[k] is None else sums[k] + term
            for k in range(blocks):
                store(k, rows, cols, sums[k])
            return carry

        lax.fori_loop(0, BLOCK // TILE * per_row, step, 0)

    def from_recv(j, s, place):
        return lambda rows, cols: recvs[j][s, place, rows, cols]

    def own_weight(e):
        return lambda k: own_w[e * blocks + k]

    def totals(j, terms, near=(-1, 0, 1)):
        def base(k, rows, cols):
            if 0 not in near:
                return tots[j][k, rows, cols]
            return pays[j][k, rows, cols].astype(jnp.float32)

        def store(k, rows, cols, value):
            tots[j][k, rows, cols] = value

        messages = []
        for a in terms:
            for s, (b, c) in enumerate(PLANE):
                if b in near:
                    messages.append((from_recv(j, s, a + 1), own_weight(number(a, b, c))))
            if a != 0 and 0 in near:

                def read(rows, cols, a=a):
                    return parts[j][slot(a), maps[slot(a), 0, number(a, 0, 0)], rows, cols]

                messages.append((read, own_weight(number(a, 0, 0))))
        accumulate(widths[j], base, messages, store)

    for j in far:
        stage(j, False)

    for e, (a, b, c) in enumerate(DIRS):
        alive = inside(-b, -c)
        for k in range(blocks):
            hit = (map_ref[25 - e] == k) & alive
            own_w[e * blocks + k] = jnp.where(hit, 1.0, 0.0).astype(jnp.float32)
    for s, (b, c) in enumerate(PLANE):

        @pl.when(jnp.logical_not(inside(-b, -c)))
        def _(s=s):
            for recv in recvs:
                recv[s] = jnp.zeros(recv.shape[1:], recv.dtype)

    for a in shifts:
        map_copy(a).wait_recv()
        mover = pltpu.make_async_copy(map_in.at[slot(a)], maps.at[slot(a)], mapc_sem.at[slot(a)])
        mover.start()
        mover.wait()
    for a in (-1, 1):
        for b in (-1, 0, 1):
            for c in (-1, 0, 1):
                e = number(a, b, c)
                alive = inside(-b, -c)
                for k in range(blocks):
                    hit = (maps[slot(-a), 0, 25 - e] == k) & alive
                    relay_w[e * blocks + k] = jnp.where(hit, 1.0, 0.0).astype(jnp.float32)

    def relay(j):
        i = far.index(j)
        arrived(j)
        for target in shifts:
            messages = []
            for a in (-1, 1):
                if slot(a) != slot(target):
                    continue
                for s, (b, c) in enumerate(PLANE):
                    e = number(a, b, c)
                    messages.append(
                        (from_recv(j, s, a + 1), lambda k, e=e: relay_w[e * blocks + k])
                    )
                e = number(a, 0, 0)

                def read(rows, cols, e=e):
                    return pays[j][map_ref[e], rows, cols]

                messages.append((read, lambda k, e=e: relay_w[e * blocks + k]))

            def store(k, rows, cols, value, target=target):
                comb[i, slot(target), k, rows, cols] = value.astype(jnp.bfloat16)

            accumulate(widths[j], lambda k, rows, cols: None, messages, store)
            b_copy(i, target).start()

    for a in shifts:
        x_copy(0, a, 0, blocks, 0).wait_recv()
    stage(0, True)
    relay(far[0])
    for a in shifts:
        for g in range(groups):
            x_copy(1, a, 2 * g, 2, g).wait_recv()
    stage(1, True)
    relay(far[1])
    totals(far[0], (0,))
    for a in shifts:
        x_copy(2, a, 0, blocks, 0).wait_recv()
    stage(2, True)
    totals(far[1], (0,))

    counts = []
    for k in range(blocks):
        count = jnp.float32(1.0)
        for e in range(26):
            count = count + own_w[e * blocks + k]
        counts.append(count)

    def split(value):
        high = value.astype(jnp.bfloat16)
        low = (value - high.astype(jnp.float32)).astype(jnp.bfloat16)
        return high, low

    arrived(0)
    totals(0, (-1, 0, 1))
    for k in range(blocks):
        high, low = split(tots[0][k])
        coupling[k, :, :BLOCK] = high
        coupling[k, :, BLOCK:] = low

    stores = []
    for i, (j, jj) in enumerate(((1, far[0]), (2, far[1]))):
        for near in ((0,), (-1, 1)):
            arrived(j, near)
            totals(j, (-1, 0, 1), near)
        for a in shifts:
            b_copy(i, a).wait_recv()
        width = widths[j]
        for k in range(blocks):
            far_sum = tots[jj][k]
            for a in shifts:
                far_sum = far_sum + comb_in[i, slot(a), k].astype(jnp.float32)
            summed = jnp.concatenate([tots[j][k], far_sum], axis=1)
            high, low = split(summed)
            spot = pl.ds(k * BLOCK, BLOCK)
            value = jnp.dot(
                coupling[k],
                jnp.concatenate([high, high], axis=0),
                preferred_element_type=jnp.float32,
            ) + jnp.dot(
                coupling[k],
                jnp.concatenate([low, low], axis=0),
                preferred_element_type=jnp.float32,
            )
            scaleds[i][spot, :] = (value / counts[k]).astype(jnp.bfloat16)
            asms[i][spot, :] = high
        cols = pl.ds(starts[j], 2 * width)
        out = pltpu.make_async_copy(asms[i], asm_hbm.at[:, cols], store_sem.at[0, i])
        out.start()
        stores.append(out)

        def step(t, carry, i=i):
            rows = pl.ds(pl.multiple_of(t * group_rows, group_rows), group_rows)
            upds[i][rows, :] = jnp.dot(
                schur[rows, :], scaleds[i][...], preferred_element_type=jnp.float32
            ).astype(jnp.bfloat16)
            return carry

        lax.fori_loop(0, groups, step, 0)
        out = pltpu.make_async_copy(upds[i], upd_hbm.at[:, cols], store_sem.at[1, i])
        out.start()
        stores.append(out)

    for a in shifts:
        map_copy(a).wait_send()
        x_copy(0, a, 0, blocks, 0).wait_send()
        for g in range(groups):
            x_copy(1, a, 2 * g, 2, g).wait_send()
        x_copy(2, a, 0, blocks, 0).wait_send()
        for i in range(2):
            b_copy(i, a).wait_send()
    for s, (b, c) in enumerate(PLANE):

        @pl.when(inside(b, c))
        def _(s=s):
            for j in range(len(widths)):
                plane_copy(j, s).wait_send()

    for out in stores:
        out.wait()


def local(sizes, schur, block_map, vectors):
    matrix = schur[0, 0, 0]
    right_side = vectors[0, 0, 0]
    links = block_map[0, 0, 0]
    order, rhs = right_side.shape
    blocks = order // BLOCK
    groups = order // (2 * BLOCK)
    bf16, f32, i32 = jnp.bfloat16, jnp.float32, jnp.int32
    share = rhs // 4
    widths = (BLOCK, share, share, share, share)
    starts = (0, 0, 2 * share, share, 3 * share)
    chunks = len(widths)
    near = 1 if sizes[0] == 2 else 2
    vmem, dma = pltpu.VMEM, pltpu.SemaphoreType.DMA
    scratch = [
        vmem((order, order), bf16),
        vmem((order, rhs), bf16),
        pltpu.SMEM((26 * blocks,), f32),
        pltpu.SMEM((26 * blocks,), f32),
        pltpu.SMEM((near, 8, 128), i32),
        vmem((8, 128), i32),
        vmem((near, 8, 128), i32),
        [vmem((blocks, BLOCK, w), bf16) for w in widths],
        [vmem((near, blocks, BLOCK, w), bf16) for w in widths[:3]],
        [vmem((8, 3, BLOCK, w), bf16) for w in widths],
        [vmem((8, 3, BLOCK, w), bf16) for w in widths],
        vmem((2, near, blocks, BLOCK, share), bf16),
        vmem((2, near, blocks, BLOCK, share), bf16),
        [vmem((blocks, BLOCK, w), f32) for w in widths],
        vmem((blocks, BLOCK, 2 * BLOCK), bf16),
        [vmem((order, 2 * share), bf16) for _ in range(2)],
        [vmem((order, 2 * share), bf16) for _ in range(2)],
        [vmem((order, 2 * share), bf16) for _ in range(2)],
        dma((blocks,)),
        dma((groups + 1,)),
        dma((2, 2)),
        dma((near,)),
        dma((near,)),
        dma((near,)),
        dma((3, near, groups)),
        dma((3, near, groups)),
        dma((chunks, 8)),
        dma((chunks, 8)),
        dma((2, near)),
        dma((2, near)),
    ]
    anywhere = pl.BlockSpec(memory_space=pl.ANY)
    assembled, update = pl.pallas_call(
        functools.partial(kernel, sizes, widths, starts),
        out_shape=[jax.ShapeDtypeStruct((order, rhs), bf16)] * 2,
        in_specs=[pl.BlockSpec(memory_space=pltpu.SMEM), anywhere, anywhere],
        out_specs=[anywhere, anywhere],
        scratch_shapes=scratch,
        compiler_params=pltpu.CompilerParams(
            collective_id=0, has_side_effects=True, vmem_limit_bytes=51 * 1024 * 1024
        ),
    )(links, matrix, right_side)
    return assembled[None, None, None], update[None, None, None]


def solution(mesh):
    placed = (
        P("gx", "gy", "gz", None, None),
        P("gx", "gy", "gz", None),
        P("gx", "gy", "gz", None, None),
    )
    sizes = tuple(mesh.shape[name] for name in ("gx", "gy", "gz"))
    return jax.shard_map(
        functools.partial(local, sizes),
        mesh=mesh,
        in_specs=placed,
        out_specs=(P("gx", "gy", "gz", None, None), P("gx", "gy", "gz", None, None)),
        check_vma=False,
    )
```
